32 devices in a mesh: dp: 8 (over z, core), tensor: 4 (over y, x).
Axes of the slice: x: 2, y: 2, z: 4, core: 2. Of those that a mesh axis runs over, the one named last changes fastest.
Arguments:
- block_input: bfloat16 [8192, 2048], P(('dp', 'tensor')), may hold values from -60 to 60
- norm_gain: float32 [2048], replicated, may hold values from 0.5 to 1.5
- norm_shift: float32 [2048], replicated, may hold values from -1.8 to 1.8
- qkv_weight: bfloat16 [3, 2048, 2048], P(None, None, 'tensor'), may hold values from -1 to 1
- qkv_bias: float32 [3, 2048], P(None, 'tensor'), may hold values from -1.8 to 1.8
- dense_weight: bfloat16 [2048, 2048], P('tensor'), may hold values from -1.5 to 1.5
- dense_bias: float32 [2048], replicated, may hold values from -1.8 to 1.8
- fc1_weight: bfloat16 [2048, 8192], P(None, 'tensor'), may hold values from -0.125 to 0.125
- fc1_bias: float32 [8192], P('tensor'), may hold values from -1.8 to 1.8
- fc2_weight: bfloat16 [8192, 2048], P('tensor'), may hold values from -0.0625 to 0.0625
- fc2_bias: float32 [2048], replicated, may hold values from -1.8 to 1.8
- cotangent: bfloat16 [8192, 2048], P(('dp', 'tensor')), may hold values from -6 to 6
Outputs:
- block_output: bfloat16 [8192, 2048], P(('dp', 'tensor'))
- input_grad: float32 [8192, 2048], P(('dp', 'tensor'))
- grad_norm_gain: float32 [2048], replicated
- grad_norm_shift: float32 [2048], replicated
- grad_qkv_weight: float32 [3, 2048, 2048], P(None, None, 'tensor')
- grad_qkv_bias: float32 [3, 2048], P(None, 'tensor')
- grad_dense_weight: float32 [2048, 2048], P('tensor')
- grad_dense_bias: float32 [2048], replicated
- grad_fc1_weight: float32 [2048, 8192], P(None, 'tensor')
- grad_fc1_bias: float32 [8192], P('tensor')
- grad_fc2_weight: float32 [8192, 2048], P('tensor')
- grad_fc2_bias: float32 [2048], replicated
The draws below stay inside these ranges and needn't reach their ends.
All inputs are finite; a program needn't handle non-finite values.
Results may differ from the reference program's by a relative error of at most 0.0099.
Values may be sent and summed in bfloat16 or wider, within the bound.
No kernel may reach another device: no remote copies, remote signals or barrier semaphores. Data moves between devices by JAX's collectives and lax.ppermute only.
A program may use at most 320 MiB of HBM per device.

```python
import math
import jax
import jax.numpy as jnp
from jax import lax

D = 2048
NH = 32
HD = 64
ROT = 32
FF = 8192
LEN = 1024
TOKENS = 8192
N_DP = 8


def draw_block_input(key, part):
    base = jax.random.truncated_normal(jax.random.fold_in(key, 1), -6.0, 6.0, (TOKENS, D), jnp.float32)
    col_scale = jnp.exp(jax.random.uniform(jax.random.fold_in(key, 2), (1, D), jnp.float32, 0.0, math.log(10.0)))
    return (base * col_scale).astype(jnp.bfloat16)


def draw_qkv_weight(key, part):
    return (jax.random.truncated_normal(jax.random.fold_in(key, 3), -6.0, 6.0, (3, D, D), jnp.float32) * D ** (-0.5)).astype(jnp.bfloat16)


def block_scale(key, shape, split, least, largest):
    def one(position, parts):
        heights = jax.random.uniform(jax.random.fold_in(jax.random.fold_in(key, 6), position), (parts,), jnp.float32, least / len(split), largest / len(split))
        return jnp.repeat(jnp.exp(heights), shape[position] // parts).reshape((-1,) + (1,) * (len(shape) - position - 1))

    loudness = one(*split[0])
    for cut in split[1:]:
        loudness = loudness * one(*cut)
    return loudness


def scatter_about(stream_key, extent, deviation, reach, shards=(), kind=jnp.bfloat16):
    gain = block_scale(stream_key, extent, shards, -0.22, 0.18) if shards else 1.0
    entries = jax.random.normal(stream_key, extent, jnp.float32) * deviation * gain
    return jnp.minimum(jnp.maximum(entries, -reach), reach).astype(kind)


def setup_inputs(seed: int = 0) -> dict:
    splits = jax.random.split(jax.random.key(seed), 13)
    block_input = draw_block_input(jax.random.fold_in(splits[12], 71), 0)
    norm_gain = jnp.clip(1.0 + 0.1 * jax.random.normal(splits[1], (D,), jnp.float32), 0.5, 1.5)
    norm_shift = scatter_about(splits[2], (D,), 0.3, 1.8, (), jnp.float32)
    qkv_weight = draw_qkv_weight(jax.random.fold_in(splits[12], 71), 0)
    qkv_bias = scatter_about(splits[4], (3, D), 0.3, 1.8, ((1, 4),), jnp.float32)
    dense_weight = scatter_about(splits[5], (D, D), (max(D // 128, 4)) ** -0.5, 1.5, ((0, 4),))
    dense_bias = scatter_about(splits[6], (D,), 0.3, 1.8, (), jnp.float32)
    fc1_weight = scatter_about(splits[7], (D, FF), D ** -0.5, 0.125, ((1, 4),))
    fc1_bias = scatter_about(splits[8], (FF,), 0.3, 1.8, ((0, 4),), jnp.float32)
    fc2_weight = scatter_about(splits[9], (FF, D), FF ** -0.5, 0.0625, ((0, 4),))
    fc2_bias = scatter_about(splits[10], (D,), 0.3, 1.8, (), jnp.float32)
    cotangent = scatter_about(splits[11], (TOKENS, D), 1.0, 6.0, ((0, 32),))
    return {"block_input": block_input, "norm_gain": norm_gain, "norm_shift": norm_shift, "qkv_weight": qkv_weight, "qkv_bias": qkv_bias, "dense_weight": dense_weight, "dense_bias": dense_bias, "fc1_weight": fc1_weight, "fc1_bias": fc1_bias, "fc2_weight": fc2_weight, "fc2_bias": fc2_bias, "cotangent": cotangent}


norm_eps = 1e-05
gelu_scale = math.sqrt(2.0 / math.pi)
gelu_cubic = 0.044715
masked_value = -1e+30

def rope_tables(length):
    halfway = ROT // 2
    inverse = 10000.0 ** (-(2.0 * jnp.arange(halfway, dtype=jnp.float32)) / ROT)
    angles = jnp.arange(length, dtype=jnp.float32)[:, None] * inverse[None, :]
    angles = jnp.concatenate([angles, angles], axis=1)
    return (jnp.cos(angles), jnp.sin(angles))

def rotate(inputs, cosine_table, sine_table):
    halfway = ROT // 2
    rotary = inputs[..., :ROT]
    turned = jnp.concatenate([-rotary[..., halfway:], rotary[..., :halfway]], axis=-1)
    mixed = rotary * cosine_table[:, None, :] + turned * sine_table[:, None, :]
    return jnp.concatenate([mixed, inputs[..., ROT:]], axis=-1)

def rotate_back(grads, cosine_table, sine_table):
    halfway = ROT // 2
    rotary = grads[..., :ROT]
    scaled = rotary * sine_table[:, None, :]
    turned = jnp.concatenate([scaled[..., halfway:], -scaled[..., :halfway]], axis=-1)
    mixed = rotary * cosine_table[:, None, :] + turned
    return jnp.concatenate([mixed, grads[..., ROT:]], axis=-1)

def gelu_parts(pre_act):
    inner = gelu_scale * (pre_act + gelu_cubic * pre_act * pre_act * pre_act)
    tangent = jnp.tanh(inner)
    value = 0.5 * pre_act * (1.0 + tangent)
    slope = 0.5 * (1.0 + tangent) + 0.5 * pre_act * (1.0 - tangent * tangent) * gelu_scale * (1.0 + 3.0 * gelu_cubic * pre_act * pre_act)
    return (value, slope)

def norm_forward(inputs, norm_gain, norm_shift):
    widened = inputs.astype(jnp.float32)
    row_mean = lax.optimization_barrier(jnp.mean(widened, axis=-1, keepdims=True))
    centred = widened - row_mean
    variance = lax.optimization_barrier(jnp.mean(centred * centred, axis=-1, keepdims=True))
    inv_std = lax.rsqrt(variance + norm_eps)
    normed = centred * inv_std
    return (normed, inv_std, (normed * norm_gain + norm_shift).astype(jnp.bfloat16))

def causal_scores(q_block, keys_all, offset):
    length = keys_all.shape[0]
    row_count = q_block.shape[0]
    scores = jnp.einsum('qhd,khd->hqk', q_block.astype(jnp.float32), keys_all.astype(jnp.float32)) * HD ** (-0.5)
    query_pos = offset + jnp.arange(row_count)
    key_pos = jnp.arange(length)
    allowed = key_pos[None, :] <= query_pos[:, None]
    return jnp.where(allowed[None], scores, masked_value)

def reference(block_input, norm_gain, norm_shift, qkv_weight, qkv_bias, dense_weight, dense_bias, fc1_weight, fc1_bias, fc2_weight, fc2_bias, cotangent):
    seq_inputs = block_input.reshape(N_DP, LEN, D)
    seq_cots = cotangent.reshape(N_DP, LEN, D)
    cosine_table, sine_table = rope_tables(LEN)
    block_len = min(512, LEN)
    block_count = LEN // block_len
    qkv_f = qkv_weight.astype(jnp.float32)

    def one_sequence(totals, seq_pair):
        inputs, upstream = seq_pair
        normed, inv_std, ln_out = norm_forward(inputs, norm_gain, norm_shift)
        projected = jnp.einsum('td,jdc->jtc', ln_out.astype(jnp.float32), qkv_f) + qkv_bias[:, None, :]
        queries = rotate(projected[0].reshape(LEN, NH, HD), cosine_table, sine_table).astype(jnp.bfloat16)
        keys_all = rotate(projected[1].reshape(LEN, NH, HD), cosine_table, sine_table).astype(jnp.bfloat16)
        values_all = projected[2].reshape(LEN, NH, HD).astype(jnp.bfloat16)
        log_totals = []
        contexts = []
        for index in range(block_count):
            offset = index * block_len
            q_block = queries[offset:offset + block_len]
            scores = causal_scores(q_block, keys_all, offset)
            row_max = lax.optimization_barrier(jnp.max(scores, axis=-1, keepdims=True))
            log_total = row_max + jnp.log(lax.optimization_barrier(jnp.sum(jnp.exp(scores - row_max), axis=-1, keepdims=True)))
            probs_b = jnp.exp(scores - log_total).astype(jnp.bfloat16)
            ctx_block = jnp.einsum('hqk,khd->qhd', probs_b.astype(jnp.float32), values_all.astype(jnp.float32))
            log_totals.append(log_total)
            contexts.append(ctx_block.astype(jnp.bfloat16))
        context = jnp.concatenate(contexts, axis=0).reshape(LEN, D)
        pre_act = jnp.dot(ln_out, fc1_weight, preferred_element_type=jnp.float32) + fc1_bias
        act_value, act_slope = gelu_parts(pre_act)
        act_b = act_value.astype(jnp.bfloat16)
        branches = jnp.dot(context, dense_weight, preferred_element_type=jnp.float32) + jnp.dot(act_b, fc2_weight, preferred_element_type=jnp.float32)
        output = (inputs.astype(jnp.float32) + branches + dense_bias + fc2_bias).astype(jnp.bfloat16)
        cot_f = upstream.astype(jnp.float32)
        grad_out_bias = lax.optimization_barrier(jnp.sum(cot_f, axis=0))
        grad_fc2_w = jnp.dot(act_b.T, upstream, preferred_element_type=jnp.float32)
        d_pre = jnp.dot(upstream, fc2_weight.T, preferred_element_type=jnp.float32) * act_slope
        grad_fc1_b = lax.optimization_barrier(jnp.sum(d_pre, axis=0))
        d_pre_b = d_pre.astype(jnp.bfloat16)
        grad_fc1_w = jnp.dot(ln_out.T, d_pre_b, preferred_element_type=jnp.float32)
        d_ln_mlp = jnp.dot(d_pre_b, fc1_weight.T, preferred_element_type=jnp.float32)
        grad_dense_w = jnp.dot(context.T, upstream, preferred_element_type=jnp.float32)
        d_context = jnp.dot(upstream, dense_weight.T, preferred_element_type=jnp.float32).astype(jnp.bfloat16).reshape(LEN, NH, HD)
        d_keys = jnp.zeros((LEN, NH, HD), jnp.float32)
        d_values = jnp.zeros((LEN, NH, HD), jnp.float32)
        d_query_list = []
        for index in range(block_count):
            offset = index * block_len
            q_block = queries[offset:offset + block_len]
            scores = causal_scores(q_block, keys_all, offset)
            attn_probs = jnp.exp(scores - log_totals[index])
            probs_b = attn_probs.astype(jnp.bfloat16)
            grad_block = d_context[offset:offset + block_len].astype(jnp.float32)
            d_probs = jnp.einsum('qhd,khd->hqk', grad_block, values_all.astype(jnp.float32))
            row_dot = lax.optimization_barrier(jnp.sum(attn_probs * d_probs, axis=-1, keepdims=True))
            d_scores = (attn_probs * (d_probs - row_dot) * HD ** (-0.5)).astype(jnp.bfloat16).astype(jnp.float32)
            d_query_list.append(jnp.einsum('hqk,khd->qhd', d_scores, keys_all.astype(jnp.float32)))
            d_keys = d_keys + jnp.einsum('hqk,qhd->khd', d_scores, q_block.astype(jnp.float32))
            d_values = d_values + jnp.einsum('hqk,qhd->khd', probs_b.astype(jnp.float32), grad_block)
        d_queries = jnp.concatenate(d_query_list, axis=0)
        d_proj = jnp.stack([rotate_back(d_queries, cosine_table, sine_table).reshape(LEN, D), rotate_back(d_keys, cosine_table, sine_table).reshape(LEN, D), d_values.reshape(LEN, D)])
        grad_qkv_b = lax.optimization_barrier(jnp.sum(d_proj, axis=1))
        d_proj_b = d_proj.astype(jnp.bfloat16).astype(jnp.float32)
        grad_qkv_w = jnp.einsum('td,jtc->jdc', ln_out.astype(jnp.float32), d_proj_b)
        d_ln = d_ln_mlp + jnp.einsum('jtc,jdc->td', d_proj_b, qkv_f)
        grad_gain = lax.optimization_barrier(jnp.sum(d_ln * normed, axis=0))
        grad_shift = lax.optimization_barrier(jnp.sum(d_ln, axis=0))
        d_normed = d_ln * norm_gain
        d_inputs = inv_std * (d_normed - lax.optimization_barrier(jnp.mean(d_normed, axis=-1, keepdims=True)) - normed * lax.optimization_barrier(jnp.mean(d_normed * normed, axis=-1, keepdims=True)))
        input_grad = cot_f + d_inputs
        grads = (grad_gain, grad_shift, grad_qkv_w, grad_qkv_b, grad_dense_w, grad_out_bias, grad_fc1_w, grad_fc1_b, grad_fc2_w, grad_out_bias)
        new_totals = tuple((left + right for left, right in zip(totals, grads)))
        return (new_totals, (output, input_grad))
    zeros_init = (jnp.zeros((D,), jnp.float32), jnp.zeros((D,), jnp.float32), jnp.zeros((3, D, D), jnp.float32), jnp.zeros((3, D), jnp.float32), jnp.zeros((D, D), jnp.float32), jnp.zeros((D,), jnp.float32), jnp.zeros((D, FF), jnp.float32), jnp.zeros((FF,), jnp.float32), jnp.zeros((FF, D), jnp.float32), jnp.zeros((D,), jnp.float32))
    totals, stacked = lax.scan(one_sequence, zeros_init, (seq_inputs, seq_cots))
    outputs, input_grads = stacked
    return (outputs.reshape(TOKENS, D), input_grads.reshape(TOKENS, D), totals[0], totals[1], totals[2], totals[3], totals[4], totals[5], totals[6], totals[7], totals[8], totals[9])
```

```python
import functools
import math

import jax
import jax.numpy as jnp
from jax import lax
from jax.experimental import pallas as pl
from jax.experimental.pallas import tpu as pltpu
from jax.sharding import PartitionSpec as P

HD = 64
ROT = 32

def rope_tables(length):
    half = ROT // 2
    lane = jnp.arange(128) % HD
    inverse = 10000.0 ** (-(2.0 * (lane % half).astype(jnp.float32)) / ROT)
    angles = jnp.arange(length, dtype=jnp.float32)[:, None] * inverse[None, :]
    cosine = jnp.where(lane < ROT, jnp.cos(angles), 1.0)
    sine = jnp.sin(angles)
    ahead = jnp.where(lane < half, -sine, 0.0)
    behind = jnp.where((lane >= half) & (lane < ROT), sine, 0.0)
    return cosine, ahead, behind

def attn_kernel(n_shard, length, place_ref, q_ref, k_ref, v_ref, dc_ref, cos_ref, ahead_ref, behind_ref,
                ctx_ref, dq_out, dk_out, dv_out, bias_out,
                q_s, k_s, v_s, qT_s, kT_s, vT_s, dc_s, dcT_s, ctxT_s, dqT_s, dk_s, dv_s):
    rows = length // n_shard
    half = ROT // 2
    bq = min(256, length)
    def rope(a, r, sign):
        c = cos_ref[r, :]; s1 = ahead_ref[r, :]; s2 = behind_ref[r, :]
        up = pltpu.roll(a, 128 - half, 1)
        dn = pltpu.roll(a, half, 1)
        return a * c + sign * (up * s1 + dn * s2)
    for b in range(n_shard):
        src = pl.ds(pl.multiple_of(place_ref[b] * rows, rows), rows)
        dst = pl.ds(b * rows, rows)
        q = (rope(q_ref[src, :], dst, 1.0)).astype(jnp.bfloat16) * jnp.bfloat16(HD ** -0.5)
        k = rope(k_ref[src, :], dst, 1.0).astype(jnp.bfloat16)
        v = v_ref[src, :].astype(jnp.bfloat16)
        dc = dc_ref[src, :]
        q_s[dst, :] = q
        k_s[dst, :] = k
        v_s[dst, :] = v
        dc_s[dst, :] = dc
        qT_s[:, dst] = q.T
        kT_s[:, dst] = k.T
        vT_s[:, dst] = v.T
        dcT_s[:, dst] = dc.T
    dk_s[...] = jnp.zeros_like(dk_s)
    dv_s[...] = jnp.zeros_like(dv_s)

    def head(h, _):
        lane_own = (lax.broadcasted_iota(jnp.int32, (bq, 128), 1) // HD) == h
        row_own = (lax.broadcasted_iota(jnp.int32, (128, bq), 0) // HD) == h
        hrows = pl.ds(pl.multiple_of(h * HD, HD), HD)
        zero = jnp.bfloat16(0)
        for i in range(length // bq):
            nk = (i + 1) * bq
            cols = pl.ds(i * bq, bq)
            qT = jnp.where(row_own, qT_s[:, cols], zero)
            dcT = jnp.where(row_own, dcT_s[:, cols], zero)
            s = jnp.dot(k_s[:nk, :], qT, preferred_element_type=jnp.float32)
            key = lax.broadcasted_iota(jnp.int32, (bq, bq), 0)
            qry = lax.broadcasted_iota(jnp.int32, (bq, bq), 1)
            diag = jnp.where(key <= qry, s[nk - bq:, :], -1e30)
            s = jnp.concatenate([s[:nk - bq, :], diag], axis=0) if i else diag
            m = jnp.max(s, axis=0, keepdims=True)
            e = jnp.exp(s - m)
            inv = 1.0 / jnp.sum(e, axis=0, keepdims=True)
            p = e * inv
            pb = p.astype(jnp.bfloat16)
            dp = jnp.dot(v_s[:nk, :], dcT, preferred_element_type=jnp.float32)
            rd = jnp.sum(p * dp, axis=0, keepdims=True)
            ds = (p * (dp - rd)).astype(jnp.bfloat16)
            ctxT_s[hrows, cols] = jnp.dot(vT_s[hrows, :nk], pb, preferred_element_type=jnp.float32)
            dqT_s[hrows, cols] = jnp.dot(kT_s[hrows, :nk], ds, preferred_element_type=jnp.float32) * HD ** -0.5
            qm = jnp.where(lane_own, q_s[cols, :], zero)
            dcm = jnp.where(lane_own, dc_s[cols, :], zero)
            dv_s[:nk, :] += jnp.dot(pb, dcm, preferred_element_type=jnp.float32)
            dk_s[:nk, :] += jnp.dot(ds, qm, preferred_element_type=jnp.float32)
        return 0
    lax.fori_loop(0, 128 // HD, head, 0)

    sums = [jnp.zeros((1, 128), jnp.float32) for _ in range(3)]
    for b in range(n_shard):
        dst = pl.ds(pl.multiple_of(place_ref[b] * rows, rows), rows)
        src = pl.ds(b * rows, rows)
        ctx_ref[dst, :] = ctxT_s[:, src].T.astype(jnp.bfloat16)
        gq = rope(dqT_s[:, src].T, src, -1.0)
        gk = rope(dk_s[src, :], src, -1.0)
        gv = dv_s[src, :]
        for j, (g, out) in enumerate(((gq, dq_out), (gk, dk_out), (gv, dv_out))):
            sums[j] = sums[j] + jnp.sum(g, axis=0, keepdims=True)
            out[dst, :] = g.astype(jnp.bfloat16)
    bias_out[...] = jnp.concatenate(sums + [jnp.zeros((5, 128), jnp.float32)], axis=0)

def attention(place, proj, dctx, tables, first, count):
    length, width = dctx.shape
    n_shard = place.shape[0]
    pair = lambda g, p: (0, g + first)
    full = lambda g, p: (0, 0)
    out = lambda g, p: (0, g)
    blk = pl.BlockSpec((length, 128), pair)
    tab = pl.BlockSpec((length, 128), full)
    oblk = pl.BlockSpec((length, 128), out)
    f32, bf = jnp.float32, jnp.bfloat16
    return pl.pallas_call(
        functools.partial(attn_kernel, n_shard, length),
        grid_spec=pltpu.PrefetchScalarGridSpec(
            num_scalar_prefetch=1, grid=(count,),
            in_specs=[blk, blk, blk, blk, tab, tab, tab],
            out_specs=[oblk, oblk, oblk, oblk, pl.BlockSpec((8, 128), out)],
            scratch_shapes=[pltpu.VMEM((length, 128), bf)] * 3 + [pltpu.VMEM((128, length), bf)] * 3
            + [pltpu.VMEM((length, 128), bf), pltpu.VMEM((128, length), bf)]
            + [pltpu.VMEM((128, length), f32)] * 2 + [pltpu.VMEM((length, 128), f32)] * 2),
        out_shape=[jax.ShapeDtypeStruct((length, count * 128), bf)] * 4 + [jax.ShapeDtypeStruct((8, count * 128), f32)],
        cost_estimate=pl.CostEstimate(flops=int(count * 2 * 6 * 2 * length * length * 256 * 0.625), bytes_accessed=count * length * 128 * 22, transcendentals=count * 2 * length * length),
        name="attention",
    )(place, proj[0], proj[1], proj[2], dctx, *tables)


norm_eps = 1e-05
gelu_scale = math.sqrt(2.0 / math.pi)
gelu_cubic = 0.044715


f32, bf16 = jnp.float32, jnp.bfloat16


def gelu_parts(z):
    inner = gelu_scale * (z + gelu_cubic * z * z * z)
    t = jnp.tanh(inner)
    value = 0.5 * z * (1.0 + t)
    slope = 0.5 * (1.0 + t) + 0.5 * z * (1.0 - t * t) * gelu_scale * (1.0 + 3.0 * gelu_cubic * z * z)
    return value, slope


def mm(a, b):
    return jnp.dot(a, b, preferred_element_type=f32)


def mm_t(a, b):
    return lax.dot_general(a, b, (((0,), (0,)), ((), ())), preferred_element_type=f32)


def mm_bt(a, b):
    return lax.dot_general(a, b, (((1,), (1,)), ((), ())), preferred_element_type=f32)


class Ring:
    def __init__(self, n):
        self.n = n
        order = list(range(0, n, 2)) + list(range(n - 1, 0, -2))
        self.position = [order.index(i) for i in range(n)]
        self.ahead = [(order[i], order[(i + 1) % n]) for i in range(n)]
        self.behind = [(b, a) for a, b in self.ahead]

    def up(self, a):
        return lax.ppermute(a, "tensor", self.ahead)

    def down(self, a):
        return lax.ppermute(a, "tensor", self.behind)

    def places(self):
        me = lax.axis_index("tensor")
        mine = jnp.where(me % 2 == 0, me // 2, self.n - 1 - me // 2)
        return (jnp.array(self.position, jnp.int32) - mine.astype(jnp.int32)) % self.n

    def gather(self, a):
        n, half = self.n, a.shape[0] // 2
        blocks = {0: a}
        up, down = a, a
        for s in range(1, n // 2):
            up, down = self.up(up), self.down(down)
            blocks[n - s], blocks[s] = up, down
        top, bottom = self.up(up[:half]), self.down(down[half:])
        blocks[n // 2] = jnp.concatenate([top, bottom], axis=0)
        return jnp.concatenate([blocks[o] for o in range(n)], axis=0)

    def reduce_scatter(self, block, rows):
        n, half = self.n, rows // 2
        far = block(n // 2).astype(bf16)
        up, down = self.up(far[:half]), self.down(far[half:])
        for s in range(2, n // 2 + 1):
            o = n // 2 - s + 1
            ahead, behind = block(o), block(n - o)
            if s == 2:
                pad = jnp.zeros((rows - half, up.shape[1]), bf16)
                ahead = ahead + jnp.concatenate([up, pad], axis=0).astype(f32)
                behind = behind + jnp.concatenate([pad, down], axis=0).astype(f32)
            else:
                ahead, behind = ahead + up.astype(f32), behind + down.astype(f32)
            up, down = self.up(ahead.astype(bf16)), self.down(behind.astype(bf16))
        return block(0) + up.astype(f32) + down.astype(f32)


class Line:
    def __init__(self, n):
        self.n, self.m = n, n // 2
        self.h = self.m // 2
        self.index = lax.axis_index("dp")
        self.core, self.chip = self.index % 2, self.index // 2

    def both(self, pairs):
        return [(2 * a + c, 2 * b + c) for a, b in pairs for c in range(2)]

    def swap(self, a):
        return lax.ppermute(a, "dp", [(i, i ^ 1) for i in range(self.n)])

    def total(self, part):
        m, h = self.m, self.h
        for s in range(1, h):
            got = lax.ppermute(part, "dp", self.both([(s - 1, s), (m - s, m - 1 - s)]))
            part = (part.astype(f32) + got.astype(f32)).astype(bf16)
        if h:
            got = lax.ppermute(part, "dp", self.both([(h - 1, h), (h, h - 1)]))
            part = (part.astype(f32) + got.astype(f32)).astype(bf16)
        for s in range(h - 1, 0, -1):
            got = lax.ppermute(part, "dp", self.both([(s, s - 1), (m - 1 - s, m - s)]))
            part = jnp.where((self.chip == s - 1) | (self.chip == m - s), got, part)
        return part

    def small(self, a):
        step = 1
        while step < self.n:
            a = a + lax.ppermute(a, "dp", [(i, i ^ step) for i in range(self.n)])
            step *= 2
        return a

    def own_first(self, a, axis):
        low, high = jnp.split(a, 2, axis=axis)
        first = self.core == 0
        return jnp.concatenate([jnp.where(first, low, high), jnp.where(first, high, low)], axis=axis)


def small_tensor(a, n):
    step = 1
    while step < n:
        a = a + lax.ppermute(a, "tensor", [(i, i ^ step) for i in range(n)])
        step *= 2
    return a


def shards(n_dp, n_tensor, block_input, norm_gain, norm_shift, qkv_weight, qkv_bias, dense_weight, dense_bias, fc1_weight, fc1_bias, fc2_weight, fc2_bias, cotangent):
    ring, line = Ring(n_tensor), Line(n_dp)
    rows, width = block_input.shape
    length = rows * n_tensor
    local = qkv_weight.shape[2]
    hidden = fc1_weight.shape[1]

    wide = block_input.astype(f32)
    centred = wide - jnp.mean(wide, axis=-1, keepdims=True)
    inv_std = lax.rsqrt(jnp.mean(centred * centred, axis=-1, keepdims=True) + norm_eps)
    normed = centred * inv_std
    ln_own = (normed * norm_gain + norm_shift).astype(bf16)
    ln = ring.gather(ln_own)
    cot = ring.gather(cotangent)
    place = ring.places()
    tables = rope_tables(length)

    own = line.own_first
    qkv_w, dense_w, fc1_w, fc2_w, fc1_b, qkv_b = lax.optimization_barrier(
        (own(qkv_weight, 2), own(dense_weight, 0), own(fc1_weight, 1), own(fc2_weight, 0), own(fc1_bias, 0), own(qkv_bias, 1))
    )

    pre = mm(ln, fc1_w) + fc1_b
    act, slope = gelu_parts(pre)
    act, slope = lax.optimization_barrier((act.astype(bf16), slope.astype(bf16)))

    def wgrad(name, terms):
        others = [line.swap(t(1).astype(bf16)) for t in terms]
        sums = [(t(0) + o.astype(f32)).astype(bf16) for t, o in zip(terms, others)]
        totals = [line.total(s) for s in sums]
        return totals, [line.swap(t) for t in totals]

    def join(totals, axis, half_axis):
        mine, theirs = (jnp.concatenate(t, axis=axis) for t in totals)
        first = line.core == 0
        low, high = jnp.where(first, mine, theirs), jnp.where(first, theirs, mine)
        return jnp.concatenate([low, high], axis=half_axis).astype(f32)

    hh = hidden // 2
    pieces = 4
    fc2_rows = hh // pieces
    fc2_terms = [
        lambda s, k=k: mm_t(act[:, s * hh + k * fc2_rows : s * hh + (k + 1) * fc2_rows], cot) for k in range(pieces)
    ]
    grad_fc2 = wgrad("fc2", fc2_terms)

    d_pre = mm_bt(cot, fc2_w) * slope.astype(f32)
    fc1_b_part = jnp.sum(d_pre, axis=0)
    d_pre = d_pre.astype(bf16)
    fc1_rows = width // pieces
    fc1_terms = [
        lambda s, k=k: mm_t(ln[:, k * fc1_rows : (k + 1) * fc1_rows], d_pre[:, s * hh : (s + 1) * hh]) for k in range(pieces)
    ]
    grad_fc1 = wgrad("fc1", fc1_terms)

    proj = [mm(ln, qkv_w[j]) + qkv_b[j] for j in range(3)]
    d_ctx = mm_bt(cot, dense_w).astype(bf16)
    pairs = local // 128
    groups = [attention(place, proj, d_ctx, tables, g, 1) for g in range(pairs)]
    ctx, dq, dk, dv = (jnp.concatenate([g[j] for g in groups], axis=1) for j in range(4))
    qkv_b_part = jnp.concatenate([g[4][:3] for g in groups], axis=1)
    d_proj = [dq, dk, dv]

    hw = local // 2
    qkv_terms = [lambda s, j=j: mm_t(ln, d_proj[j][:, s * hw : (s + 1) * hw]) for j in range(3)]
    grad_qkv = wgrad("qkv", qkv_terms)
    dense_terms = [lambda s: mm_t(ctx[:, s * hw : (s + 1) * hw], cot)]
    grad_dense = wgrad("dense", dense_terms)

    def d_ln_block(o):
        r = slice(o * rows, (o + 1) * rows)
        return mm_bt(d_pre[r], fc1_w) + mm_bt(dq[r], qkv_w[0]) + mm_bt(dk[r], qkv_w[1]) + mm_bt(dv[r], qkv_w[2])

    d_ln = ring.reduce_scatter(d_ln_block, rows)

    def branch_block(o):
        r = slice(o * rows, (o + 1) * rows)
        return mm(ctx[r], dense_w) + mm(act[r], fc2_w)

    branches = ring.reduce_scatter(branch_block, rows)
    block_output = (wide + branches + dense_bias + fc2_bias).astype(bf16)

    cot_own = cotangent.astype(f32)
    d_normed = d_ln * norm_gain
    input_grad = cot_own + inv_std * (
        d_normed
        - jnp.mean(d_normed, axis=-1, keepdims=True)
        - normed * jnp.mean(d_normed * normed, axis=-1, keepdims=True)
    )
    vectors = jnp.stack([jnp.sum(d_ln * normed, axis=0), jnp.sum(d_ln, axis=0), jnp.sum(cot_own, axis=0)])
    grad_gain, grad_shift, grad_out_bias = line.small(small_tensor(vectors, n_tensor))
    biases = line.small(jnp.concatenate([own(fc1_b_part, 0), own(qkv_b_part, 1).reshape(-1)]))
    grad_fc1_b = biases[:hidden]
    grad_qkv_b = biases[hidden:].reshape(3, local)

    grad_fc2_w = join(grad_fc2, 0, 0)
    grad_fc1_w = join(grad_fc1, 0, 1)
    grad_qkv_w = join([[t[None] for t in g] for g in grad_qkv], 0, 2)
    grad_dense_w = join(grad_dense, 0, 0)
    return (
        block_output,
        input_grad,
        grad_gain,
        grad_shift,
        grad_qkv_w,
        grad_qkv_b,
        grad_dense_w,
        grad_out_bias,
        grad_fc1_w,
        grad_fc1_b,
        grad_fc2_w,
        grad_out_bias,
    )


def solution(mesh):
    n_dp, n_tensor = mesh.shape["dp"], mesh.shape["tensor"]
    token = P(("dp", "tensor"), None)
    weights = (P(None, None, "tensor"), P(None, "tensor"), P("tensor", None), P(), P(None, "tensor"), P("tensor"), P("tensor", None), P())
    return jax.shard_map(
        functools.partial(shards, n_dp, n_tensor),
        mesh=mesh,
        in_specs=(token, P(), P()) + weights + (token,),
        out_specs=(token, token, P(), P()) + weights,
        check_vma=False,
    )
```
